32 devices in a mesh: section: 2 (over x), row: 4 (over y, core), col: 4 (over z).
Axes of the slice: x: 2, y: 2, z: 4, core: 2. Of those that a mesh axis runs over, the one named last changes fastest.
Arguments:
- layer_input: bfloat16 [2, 2, 128, 8192], P('section', None, 'col', 'row'), may hold values from -6 to 6
- top_grad: bfloat16 [2, 128, 8192], P(None, 'col', 'row'), may hold values from -6 to 6
- gate_weight: bfloat16 [2, 8192, 14336], P('section', 'row', 'col'), may hold values from -0.0625 to 0.0625
- up_weight: bfloat16 [2, 8192, 14336], P('section', 'row', 'col'), may hold values from -0.0625 to 0.0625
- down_weight: bfloat16 [2, 14336, 8192], P('section', 'col', 'row'), may hold values from -0.046875 to 0.046875
- activity: int32 [2, 2, 2, 4, 28], P('section', None, None, 'col'), may hold values from 0 to 56, as said below
Outputs:
- sent_grad: bfloat16 [2, 2, 128, 8192], P('section', None, 'col', 'row')
- gate_grad: bfloat16 [2, 8192, 14336], P('section', 'row', 'col')
- up_grad: bfloat16 [2, 8192, 14336], P('section', 'row', 'col')
- down_grad: bfloat16 [2, 14336, 8192], P('section', 'col', 'row')
The draws below stay inside these ranges and needn't reach their ends.
Inputs may be any that keep to these rules, and one draw needn't show every extreme that they name: `activity`: each list names distinct blocks below 56, then the value 56 marks empty slots up to the end; every list holds at least 7 blocks, and in every token block some column's list is full.
All inputs are finite; a program needn't handle non-finite values.
Results may differ from the reference program's by a relative error of at most 0.006.
Values may be sent and summed in bfloat16 or wider, within the bound.
No kernel may reach another device: no remote copies, remote signals or barrier semaphores. Data moves between devices by JAX's collectives and lax.ppermute only.
A program may use at most 384 MiB of HBM per device.

```python
import jax
import jax.numpy as jnp

D = 8192
FF = 14336
BLK = 64
TB = 64
TOK = 128
MICRO = 2
LAYERS = 2
TBLK = 2
NBC = 56
KACT = 28
N_COL = 4


def draw_activity(key, part):
    row_total = LAYERS * MICRO * TBLK * N_COL
    row_keys = jax.random.split(jax.random.fold_in(key, 7), row_total)
    orders = jax.vmap(lambda one_key: jax.random.permutation(one_key, NBC))(row_keys)[:, :KACT]
    counts = jax.random.randint(jax.random.fold_in(key, 9), (row_total,), max(1, KACT // 4), KACT + 1)
    row_index = jnp.arange(row_total, dtype=jnp.int32)
    column = row_index % N_COL
    group = row_index // N_COL
    counts = jnp.where(column == group % N_COL, KACT, counts)
    slot_index = jnp.arange(KACT, dtype=jnp.int32)
    lists = jnp.where(slot_index[None, :] < counts[:, None], orders.astype(jnp.int32), NBC)
    return lists.astype(jnp.int32).reshape(LAYERS, MICRO, TBLK, N_COL, KACT)


def block_levels(rng, extent, shards, least, largest):
    def one(position, shards_of):
        steps = jax.random.uniform(jax.random.fold_in(jax.random.fold_in(rng, 6), position), (shards_of,), jnp.float32, least / len(shards), largest / len(shards))
        return jnp.repeat(jnp.exp(steps), extent[position] // shards_of).reshape((-1,) + (1,) * (len(extent) - position - 1))

    factor_of = one(*shards[0])
    for cut in shards[1:]:
        factor_of = factor_of * one(*cut)
    return factor_of


def noise(key, shape, width, bound, cuts=(), held_as=jnp.bfloat16):
    level = block_levels(key, shape, cuts, -0.22, 0.18) if cuts else 1.0
    result = jax.random.normal(key, shape, jnp.float32) * width * level
    return jnp.minimum(jnp.maximum(result, -bound), bound).astype(held_as)


def setup_inputs(seed: int = 0) -> dict:
    seeds = jax.random.split(jax.random.key(seed), 7)
    layer_input = noise(seeds[0], (LAYERS, MICRO, TOK, D), 1.0, 6.0, ((0, 2), (2, 4), (3, 4)))
    top_grad = noise(seeds[1], (MICRO, TOK, D), 1.0, 6.0, ((1, 4), (2, 4)))
    gate_weight = noise(seeds[2], (LAYERS, D, FF), D ** -0.5, 0.0625, ((0, 2), (1, 4), (2, 4)))
    up_weight = noise(seeds[3], (LAYERS, D, FF), D ** -0.5, 0.0625, ((0, 2), (1, 4), (2, 4)))
    down_weight = noise(seeds[4], (LAYERS, FF, D), FF ** -0.5, 0.046875, ((0, 2), (1, 4), (2, 4)))
    activity = draw_activity(jax.random.fold_in(seeds[6], 71), 0)
    return {"layer_input": layer_input, "top_grad": top_grad, "gate_weight": gate_weight, "up_weight": up_weight, "down_weight": down_weight, "activity": activity}


def block_mask(lists):
    blocks = jnp.arange(NBC, dtype=jnp.int32)
    block_on = jnp.any(lists[..., None] == blocks, axis=-2).astype(jnp.float32)
    spread = jnp.broadcast_to(block_on[:, None, :, :, None], (TBLK, TB, N_COL, NBC, BLK))
    return spread.reshape(TBLK * TB, N_COL * NBC * BLK)


def activate(gate_total, up_total, grad_total, keep_mask):
    positive = jnp.maximum(gate_total, 0.0)
    squared = keep_mask * positive * positive
    hidden = (squared * up_total).astype(jnp.bfloat16)
    grad_up = (squared * grad_total).astype(jnp.bfloat16)
    grad_hgate = (keep_mask * 2.0 * positive * up_total * grad_total).astype(jnp.bfloat16)
    return hidden, grad_hgate, grad_up


def layer_back(layer_in, grad_out, w_gate, w_up, w_down, lists):
    keep_mask = block_mask(lists)
    gate_total = jnp.dot(layer_in, w_gate, preferred_element_type=jnp.float32)
    up_total = jnp.dot(layer_in, w_up, preferred_element_type=jnp.float32)
    grad_total = jnp.dot(grad_out, w_down.T, preferred_element_type=jnp.float32)
    hidden, grad_hgate, grad_up = activate(gate_total, up_total, grad_total, keep_mask)
    down_term = jnp.dot(hidden.T, grad_out, preferred_element_type=jnp.float32)
    gate_term = jnp.dot(layer_in.T, grad_hgate, preferred_element_type=jnp.float32)
    up_term = jnp.dot(layer_in.T, grad_up, preferred_element_type=jnp.float32)
    handed = grad_out.astype(jnp.float32) + jnp.dot(grad_hgate, w_gate.T, preferred_element_type=jnp.float32)
    handed = handed + jnp.dot(grad_up, w_up.T, preferred_element_type=jnp.float32)
    return handed.astype(jnp.bfloat16), gate_term, up_term, down_term


def reference(layer_input, top_grad, gate_weight, up_weight, down_weight, activity):
    sent_layers = [None] * LAYERS
    gate_list = [None] * LAYERS
    up_list = [None] * LAYERS
    down_list = [None] * LAYERS
    for layer_index in range(LAYERS - 1, -1, -1):
        sum_gate = jnp.zeros((D, FF), jnp.float32)
        sum_up = jnp.zeros((D, FF), jnp.float32)
        sum_down = jnp.zeros((FF, D), jnp.float32)
        handed_list = []
        for micro_index in range(MICRO):
            if layer_index == LAYERS - 1:
                grad_out = top_grad[micro_index]
            else:
                grad_out = sent_layers[layer_index + 1][micro_index]
            handed, gate_term, up_term, down_term = layer_back(
                layer_input[layer_index, micro_index], grad_out, gate_weight[layer_index],
                up_weight[layer_index], down_weight[layer_index], activity[layer_index, micro_index])
            sum_gate = sum_gate + gate_term
            sum_up = sum_up + up_term
            sum_down = sum_down + down_term
            handed_list.append(handed)
        sent_layers[layer_index] = jnp.stack(handed_list)
        gate_list[layer_index] = sum_gate.astype(jnp.bfloat16)
        up_list[layer_index] = sum_up.astype(jnp.bfloat16)
        down_list[layer_index] = sum_down.astype(jnp.bfloat16)
    return (jnp.stack(sent_layers), jnp.stack(gate_list), jnp.stack(up_list), jnp.stack(down_list))
```

```python
import functools

import jax
import jax.numpy as jnp
from jax import lax
from jax.experimental import pallas as pl
from jax.experimental.pallas import tpu as pltpu
from jax.sharding import PartitionSpec as P

BLK = 64
TB = 64
CHUNKS = 2
VMEM_LIMIT = 48 * 1024 * 1024

bf16 = jnp.bfloat16
f32 = jnp.float32


def rotated(value, axis, steps):
    count = lax.axis_size(axis)
    return lax.ppermute(value, axis, [(i, (i + steps) % count) for i in range(count)])


def swapped(value, axis):
    count = lax.axis_size(axis)
    return lax.ppermute(value, axis, [(i, i ^ 1) for i in range(count)])


def gathered(value, axis):
    count = lax.axis_size(axis)
    return [value] + [rotated(value, axis, k) for k in range(1, count)]


def tile_of(extent, *choices):
    for choice in choices:
        if extent % choice == 0:
            return choice
    return extent


class Sizes:
    def __init__(self, micro, local, cols, width, hidden, slots):
        self.micro, self.local, self.cols = micro, local, cols
        self.width, self.hidden, self.slots = width, hidden, slots
        self.tok = local * cols
        self.all_tok = micro * self.tok
        self.groups = self.tok // TB
        self.blocks = hidden // BLK
        self.half = slots // 2
        self.packed = slots * BLK
        self.half_rows = self.half * BLK

    def assemble(self, pieces, dest, first=0):
        extent = pieces[0].shape[-1]
        for m in range(self.micro):
            for k in range(self.cols):
                start = m * self.tok + k * self.local
                dest[start : start + self.local, first : first + extent] = pieces[k][m]

    def pack(self, lists, lane_group, dense, mine, theirs):
        masks = [
            jnp.broadcast_to(lane_group[0:1, :] == g, (BLK, self.tok)) for g in range(1, self.groups)
        ]

        def one(j, dest):
            def step(slot, carry):
                for m in range(self.micro):
                    lanes = slice(m * self.tok, (m + 1) * self.tok)
                    value = None
                    for g in range(self.groups):
                        block = lists[(m * self.groups + g) * self.slots + j * self.half + slot]
                        rows = pl.ds(pl.multiple_of(block * BLK, BLK), BLK)
                        part = dense[rows, lanes]
                        value = part if value is None else jnp.where(masks[g - 1], part, value)
                    out_rows = pl.ds(pl.multiple_of(slot * BLK, BLK), BLK)
                    dest[out_rows, lanes] = value.astype(dest.dtype)
                return carry

            lax.fori_loop(0, self.half, step, 0)

        one(0, mine)
        one(1, theirs)

    def spread(self, places, lane_group, packed_list, dense_list):
        masks = [
            jnp.broadcast_to(lane_group[0:1, :] == g, (BLK, self.tok)) for g in range(1, self.groups)
        ]

        def step(block, carry):
            for m in range(self.micro):
                lanes = slice(m * self.tok, (m + 1) * self.tok)
                rows = []
                for g in range(self.groups):
                    place = places[(m * self.groups + g) * self.blocks + block]
                    rows.append(pl.ds(pl.multiple_of(place * BLK, BLK), BLK))
                out_rows = pl.ds(pl.multiple_of(block * BLK, BLK), BLK)
                for packed, dense in zip(packed_list, dense_list):
                    value = packed[rows[0], lanes]
                    for g in range(1, self.groups):
                        value = jnp.where(masks[g - 1], packed[rows[g], lanes], value)
                    dense[out_rows, lanes] = value
            return carry

        lax.fori_loop(0, self.blocks, step, 0)

    def join(self, mine, theirs, packed):
        packed[0 : self.half_rows, :] = mine[...]
        packed[self.half_rows : self.packed, :] = theirs[...]
        packed[self.packed : self.packed + BLK, :] = jnp.zeros((BLK, self.all_tok), packed.dtype)


def whole_spec(shape):
    zeros = (0,) * len(shape)
    return pl.BlockSpec(shape, lambda *_: zeros)


def params():
    return pltpu.CompilerParams(dimension_semantics=("arbitrary",), vmem_limit_bytes=VMEM_LIMIT)


def packed_outs(z):
    return (
        (
            jax.ShapeDtypeStruct((z.half_rows, z.all_tok), f32),
            jax.ShapeDtypeStruct((z.half_rows, z.all_tok), bf16),
        ),
        (whole_spec((z.half_rows, z.all_tok)), whole_spec((z.half_rows, z.all_tok))),
    )


def cost(z, matmuls, extra=0):
    size = z.width * z.hidden
    return pl.CostEstimate(
        flops=int(2 * z.all_tok * size * matmuls),
        bytes_accessed=int(2 * size * matmuls + extra),
        transcendentals=0,
    )


def forward_part(z, lists, lane_group, pieces, weight):
    tile = tile_of(z.hidden, 512, 256, 128)
    steps = z.hidden // tile

    def kernel(lists_ref, group_ref, *refs):
        piece_refs, (w_ref, mine, theirs, rows, dense) = refs[: z.cols], refs[z.cols :]
        i = pl.program_id(0)

        @pl.when(i == 0)
        def _():
            z.assemble(piece_refs, rows)
            dense[z.hidden : z.hidden + BLK, :] = jnp.zeros((BLK, z.all_tok), f32)

        part = jnp.dot(rows[...], w_ref[...], preferred_element_type=f32)
        dense[pl.ds(pl.multiple_of(i * tile, tile), tile), :] = part.T

        @pl.when(i == steps - 1)
        def _():
            z.pack(lists_ref, group_ref, dense, mine, theirs)

    out_shape, out_specs = packed_outs(z)
    return pl.pallas_call(
        kernel,
        out_shape=out_shape,
        grid_spec=pltpu.PrefetchScalarGridSpec(
            num_scalar_prefetch=1,
            grid=(steps,),
            in_specs=[whole_spec(lane_group.shape)]
            + [whole_spec(piece.shape) for piece in pieces]
            + [pl.BlockSpec((None, z.width, tile), lambda i, *_: (0, 0, i))],
            out_specs=out_specs,
            scratch_shapes=[
                pltpu.VMEM((z.all_tok, z.width), bf16),
                pltpu.VMEM((z.hidden + BLK, z.all_tok), f32),
            ],
        ),
        compiler_params=params(),
        cost_estimate=cost(z, 1),
    )(lists, lane_group, *pieces, weight)


def back_part(z, lists, lane_group, pieces, weight, chunk, chunks, before):
    tile = tile_of(z.hidden, 512, 256, 128)
    steps = z.hidden // tile
    extent = z.width // chunks
    last = chunk == chunks - 1

    def kernel(lists_ref, group_ref, *refs):
        piece_refs, refs = refs[: z.cols], refs[z.cols :]
        w_ref, refs = refs[0], refs[1:]
        if before is not None:
            before_ref, refs = refs[0], refs[1:]
        i = pl.program_id(0)
        rows = refs[-1] if not last else refs[-2]

        @pl.when(i == 0)
        def _():
            z.assemble(piece_refs, rows)

        part = lax.dot_general(
            w_ref[...], rows[...], (((1,), (1,)), ((), ())), preferred_element_type=f32
        )
        if before is not None:
            part = part + before_ref[...]
        if not last:
            refs[0][...] = part
        else:
            mine, theirs, _, dense = refs
            dense[pl.ds(pl.multiple_of(i * tile, tile), tile), :] = part

            @pl.when(i == steps - 1)
            def _():
                dense[z.hidden : z.hidden + BLK, :] = jnp.zeros((BLK, z.all_tok), f32)
                z.pack(lists_ref, group_ref, dense, mine, theirs)

    scratch = [pltpu.VMEM((z.all_tok, extent), bf16)]
    row_spec = pl.BlockSpec((tile, z.all_tok), lambda i, *_: (i, 0))
    if last:
        out_shape, out_specs = packed_outs(z)
        scratch.append(pltpu.VMEM((z.hidden + BLK, z.all_tok), f32))
    else:
        out_shape, out_specs = jax.ShapeDtypeStruct((z.hidden, z.all_tok), f32), row_spec
    ins = [lane_group, *pieces, weight]
    in_specs = (
        [whole_spec(lane_group.shape)]
        + [whole_spec(piece.shape) for piece in pieces]
        + [pl.BlockSpec((None, tile, extent), lambda i, *_: (0, i, chunk))]
    )
    if before is not None:
        ins.append(before)
        in_specs.append(row_spec)
    return pl.pallas_call(
        kernel,
        out_shape=out_shape,
        grid_spec=pltpu.PrefetchScalarGridSpec(
            num_scalar_prefetch=1,
            grid=(steps,),
            in_specs=in_specs,
            out_specs=out_specs,
            scratch_shapes=scratch,
        ),
        compiler_params=params(),
        cost_estimate=cost(z, 1 / chunks),
    )(lists, *ins)


def sent_part(z, places, lane_group, gate_halves, up_halves, w_gate, w_up, chunk, chunks):
    extent = z.width // chunks
    tile = tile_of(extent, 256, 128)
    steps = extent // tile

    def kernel(places_ref, group_ref, gm, gt, um, ut, wg, wu, *refs):
        outs, (packed_g, packed_u, dense_g, dense_u) = refs[: z.cols], refs[z.cols :]
        i = pl.program_id(0)

        @pl.when(i == 0)
        def _():
            z.join(gm, gt, packed_g)
            z.join(um, ut, packed_u)
            z.spread(places_ref, group_ref, [packed_g, packed_u], [dense_g, dense_u])

        part = jnp.dot(wg[...], dense_g[...], preferred_element_type=f32)
        part = part + jnp.dot(wu[...], dense_u[...], preferred_element_type=f32)
        turned = part.T
        for m in range(z.micro):
            for k in range(z.cols):
                start = m * z.tok + k * z.local
                outs[k][m] = turned[start : start + z.local, :].astype(outs[k].dtype)

    half = (z.half_rows, z.all_tok)
    w_spec = pl.BlockSpec((None, tile, z.hidden), lambda i, *_: (0, chunk * steps + i, 0))
    out_spec = pl.BlockSpec((z.micro, z.local, tile), lambda i, *_: (0, 0, i))
    return pl.pallas_call(
        kernel,
        out_shape=[
            jax.ShapeDtypeStruct((z.micro, z.local, extent), f32 if k == 0 else bf16)
            for k in range(z.cols)
        ],
        grid_spec=pltpu.PrefetchScalarGridSpec(
            num_scalar_prefetch=1,
            grid=(steps,),
            in_specs=[whole_spec(lane_group.shape)] + [whole_spec(half)] * 4 + [w_spec, w_spec],
            out_specs=[out_spec] * z.cols,
            scratch_shapes=[pltpu.VMEM((z.packed + BLK, z.all_tok), bf16)] * 2
            + [pltpu.VMEM((z.hidden, z.all_tok), bf16)] * 2,
        ),
        compiler_params=params(),
        cost_estimate=cost(z, 2 / chunks),
    )(places, lane_group, *gate_halves, *up_halves, w_gate, w_up)


def down_gradient(z, places, lane_group, halves, chunk_pieces):
    tile = tile_of(z.hidden, 512, 256, 128)
    steps = z.hidden // tile
    flat = [piece for pieces in chunk_pieces for piece in pieces]
    count = len(flat)

    def kernel(places_ref, group_ref, hm, ht, *refs):
        piece_refs, (out, packed, dense, rows) = refs[:count], refs[count:]
        i = pl.program_id(0)

        @pl.when(i == 0)
        def _():
            z.join(hm, ht, packed)
            z.spread(places_ref, group_ref, [packed], [dense])
            for n in range(len(chunk_pieces)):
                group = piece_refs[n * z.cols : (n + 1) * z.cols]
                z.assemble(group, rows, n * group[0].shape[-1])

        own = dense[pl.ds(pl.multiple_of(i * tile, tile), tile), :]
        out[...] = jnp.dot(own, rows[...], preferred_element_type=f32).astype(bf16)

    half = (z.half_rows, z.all_tok)
    return pl.pallas_call(
        kernel,
        out_shape=jax.ShapeDtypeStruct((1, z.hidden, z.width), bf16),
        grid_spec=pltpu.PrefetchScalarGridSpec(
            num_scalar_prefetch=1,
            grid=(steps,),
            in_specs=[whole_spec(lane_group.shape)]
            + [whole_spec(half)] * 2
            + [whole_spec(piece.shape) for piece in flat],
            out_specs=pl.BlockSpec((None, tile, z.width), lambda i, *_: (0, i, 0)),
            scratch_shapes=[
                pltpu.VMEM((z.packed + BLK, z.all_tok), bf16),
                pltpu.VMEM((z.hidden, z.all_tok), bf16),
                pltpu.VMEM((z.all_tok, z.width), bf16),
            ],
        ),
        compiler_params=params(),
        cost_estimate=cost(z, 1),
    )(places, lane_group, *halves, *flat)


def gate_up_gradients(z, places, lane_group, gate_halves, up_halves, pieces):
    tile = tile_of(z.width, 256, 128)
    steps = z.width // tile

    def kernel(places_ref, group_ref, gm, gt, um, ut, *refs):
        piece_refs, refs = refs[: z.cols], refs[z.cols :]
        out_g, out_u, packed_g, packed_u, dense_g, dense_u, rows = refs
        i = pl.program_id(0)

        @pl.when(i == 0)
        def _():
            z.join(gm, gt, packed_g)
            z.join(um, ut, packed_u)
            z.spread(places_ref, group_ref, [packed_g, packed_u], [dense_g, dense_u])

        z.assemble(piece_refs, rows)
        turned = rows[...].T
        dims = (((1,), (1,)), ((), ()))
        out_g[...] = lax.dot_general(
            turned, dense_g[...], dims, preferred_element_type=f32
        ).astype(bf16)
        out_u[...] = lax.dot_general(
            turned, dense_u[...], dims, preferred_element_type=f32
        ).astype(bf16)

    half = (z.half_rows, z.all_tok)
    out_spec = pl.BlockSpec((None, tile, z.hidden), lambda i, *_: (0, i, 0))
    return pl.pallas_call(
        kernel,
        out_shape=[jax.ShapeDtypeStruct((1, z.width, z.hidden), bf16)] * 2,
        grid_spec=pltpu.PrefetchScalarGridSpec(
            num_scalar_prefetch=1,
            grid=(steps,),
            in_specs=[whole_spec(lane_group.shape)]
            + [whole_spec(half)] * 4
            + [pl.BlockSpec((z.micro, z.local, tile), lambda i, *_: (0, 0, i))] * z.cols,
            out_specs=[out_spec] * 2,
            scratch_shapes=[pltpu.VMEM((z.packed + BLK, z.all_tok), bf16)] * 2
            + [pltpu.VMEM((z.hidden, z.all_tok), bf16)] * 2
            + [pltpu.VMEM((z.all_tok, tile), bf16)],
        ),
        compiler_params=params(),
        cost_estimate=cost(z, 2),
    )(places, lane_group, *gate_halves, *up_halves, *pieces)


def row_total(parts):
    mine, theirs = parts
    chip = mine + swapped(theirs, "row").astype(f32)
    outgoing = chip.astype(bf16)
    total = chip
    for step in range(2, lax.axis_size("row"), 2):
        total = total + rotated(outgoing, "row", step).astype(f32)
    return total


def shards(layer_input, top_grad, w_gate, w_up, w_down, activity):
    sections = lax.axis_size("section")
    is_last = lax.axis_index("section") == sections - 1
    cols = lax.axis_size("col")
    col = lax.axis_index("col")
    core = lax.axis_index("row") % 2
    inputs = layer_input[0]
    lists = activity[0, :, :, 0, :]
    z = Sizes(
        inputs.shape[0], inputs.shape[1], cols, inputs.shape[2], w_gate.shape[2], lists.shape[-1]
    )

    turned = jnp.where(core == 0, lists, jnp.roll(lists, -z.half, axis=-1))
    numbers = jnp.arange(z.blocks, dtype=jnp.int32)
    hit = turned[..., :, None] == numbers
    slot_ids = jnp.arange(z.slots, dtype=jnp.int32)[:, None]
    places = jnp.min(jnp.where(hit, slot_ids, z.slots), axis=-2).reshape(-1)
    turned = turned.reshape(-1)
    lane = jnp.arange(z.tok, dtype=jnp.int32)
    source = (col - lane // z.local) % cols
    group = (source * z.local + lane % z.local) // TB
    lane_group = jnp.broadcast_to(group[None], (8, z.tok))

    input_pieces = gathered(inputs, "col")
    top_pieces = gathered(top_grad, "col")
    gate = row_total(forward_part(z, turned, lane_group, input_pieces, w_gate))
    up = row_total(forward_part(z, turned, lane_group, input_pieces, w_up))
    positive = jnp.maximum(gate, 0.0)
    squared = positive * positive
    slope = 2.0 * positive * up
    hidden = (squared * up).astype(bf16)
    hidden_halves = (hidden, swapped(hidden, "row"))

    extent = z.width // CHUNKS
    spans = [slice(n * extent, (n + 1) * extent) for n in range(CHUNKS)]
    chunk_pieces = None
    own = [top_grad[:, :, span] for span in spans]
    for turn in range(sections):
        if turn == 0:
            parts = back_part(z, turned, lane_group, top_pieces, w_down, 0, 1, None)
        else:
            chunk_pieces = [gathered(value, "col") for value in own]
            parts = None
            for n in range(CHUNKS):
                parts = back_part(
                    z, turned, lane_group, chunk_pieces[n], w_down, n, CHUNKS, parts
                )
        back = row_total(parts)
        grad_gate = (slope * back).astype(bf16)
        grad_up = (squared * back).astype(bf16)
        gate_halves = (grad_gate, swapped(grad_gate, "row"))
        up_halves = (grad_up, swapped(grad_up, "row"))
        handed = []
        for n in range(CHUNKS):
            rows = sent_part(
                z, places, lane_group, gate_halves, up_halves, w_gate, w_up, n, CHUNKS
            )
            total = own[n].astype(f32) + rows[0]
            for k in range(1, cols):
                total = total + rotated(rows[k], "col", -k).astype(f32)
            handed.append(total.astype(bf16))
        if turn < sections - 1:
            pairs = [(i, i - 1) for i in range(1, sections)]
            own = [
                jnp.where(is_last, top_grad[:, :, span], lax.ppermute(value, "section", pairs))
                for span, value in zip(spans, handed)
            ]
    if chunk_pieces is None:
        chunk_pieces = [top_pieces]
    down_grad = down_gradient(z, places, lane_group, hidden_halves, chunk_pieces)
    gate_grad, up_grad = gate_up_gradients(
        z, places, lane_group, gate_halves, up_halves, input_pieces
    )
    sent = jnp.concatenate(handed, axis=-1)[None]
    return sent, gate_grad, up_grad, down_grad


def solution(mesh):
    in_specs = (
        P("section", None, "col", "row"),
        P(None, "col", "row"),
        P("section", "row", "col"),
        P("section", "row", "col"),
        P("section", "col", "row"),
        P("section", None, None, "col", None),
    )
    out_specs = (
        P("section", None, "col", "row"),
        P("section", "row", "col"),
        P("section", "row", "col"),
        P("section", "col", "row"),
    )
    return jax.shard_map(shards, mesh=mesh, in_specs=in_specs, out_specs=out_specs, check_vma=False)
```

```python
import jax
import jax.numpy as jnp
from jax import lax
from jax.experimental import pallas as pl
from jax.experimental.pallas import tpu as pltpu
from jax.sharding import PartitionSpec as P


BLK = 64
TB = 64
CHUNKS = 2
VMEM_LIMIT = 48 * 1024 * 1024

bf16 = jnp.bfloat16
f32 = jnp.float32


def rotated(value, axis, steps):
    count = lax.axis_size(axis)
    return lax.ppermute(value, axis, [(i, (i + steps) % count) for i in range(count)])


def swapped(value, axis):
    count = lax.axis_size(axis)
    return lax.ppermute(value, axis, [(i, i ^ 1) for i in range(count)])


def gathered(value, axis):
    count = lax.axis_size(axis)
    return [value] + [rotated(value, axis, k) for k in range(1, count)]


def tile_of(extent, *choices):
    for choice in choices:
        if extent % choice == 0:
            return choice
    return extent


class Sizes:
    def __init__(self, micro, local, cols, width, hidden, slots):
        self.micro, self.local, self.cols = micro, local, cols
        self.width, self.hidden, self.slots = width, hidden, slots
        self.tok = local * cols
        self.all_tok = micro * self.tok
        self.groups = self.tok // TB
        self.blocks = hidden // BLK
        self.half = slots // 2
        self.packed = slots * BLK
        self.half_rows = self.half * BLK

    def assemble(self, pieces, dest, first=0):
        extent = pieces[0].shape[-1]
        for m in range(self.micro):
            for k in range(self.cols):
                start = m * self.tok + k * self.local
                dest[start : start + self.local, first : first + extent] = pieces[k][m]

    def pack(self, lists, lane_group, dense, mine, theirs):
        masks = [
            jnp.broadcast_to(lane_group[0:1, :] == g, (BLK, self.tok)) for g in range(1, self.groups)
        ]

        def one(j, dest):
            def step(slot, carry):
                for m in range(self.micro):
                    lanes = slice(m * self.tok, (m + 1) * self.tok)
                    value = None
                    for g in range(self.groups):
                        block = lists[(m * self.groups + g) * self.slots + j * self.half + slot]
                        rows = pl.ds(pl.multiple_of(block * BLK, BLK), BLK)
                        part = dense[rows, lanes]
                        value = part if value is None else jnp.where(masks[g - 1], part, value)
                    out_rows = pl.ds(pl.multiple_of(slot * BLK, BLK), BLK)
                    dest[out_rows, lanes] = value.astype(dest.dtype)
                return carry

            lax.fori_loop(0, self.half, step, 0)

        one(0, mine)
        one(1, theirs)

    def spread(self, places, lane_group, packed_list, dense_list):
        masks = [
            jnp.broadcast_to(lane_group[0:1, :] == g, (BLK, self.tok)) for g in range(1, self.groups)
        ]

        def step(block, carry):
            for m in range(self.micro):
                lanes = slice(m * self.tok, (m + 1) * self.tok)
                rows = []
                for g in range(self.groups):
                    place = places[(m * self.groups + g) * self.blocks + block]
                    rows.append(pl.ds(pl.multiple_of(place * BLK, BLK), BLK))
                out_rows = pl.ds(pl.multiple_of(block * BLK, BLK), BLK)
                for packed, dense in zip(packed_list, dense_list):
                    value = packed[rows[0], lanes]
                    for g in range(1, self.groups):
                        value = jnp.where(masks[g - 1], packed[rows[g], lanes], value)
                    dense[out_rows, lanes] = value
            return carry

        lax.fori_loop(0, self.blocks, step, 0)

    def join(self, mine, theirs, packed):
        packed[0 : self.half_rows, :] = mine[...]
        packed[self.half_rows : self.packed, :] = theirs[...]
        packed[self.packed : self.packed + BLK, :] = jnp.zeros((BLK, self.all_tok), packed.dtype)


def whole_spec(shape):
    zeros = (0,) * len(shape)
    return pl.BlockSpec(shape, lambda *_: zeros)


def any_spec():
    return pl.BlockSpec(memory_space=pl.ANY)


def vmem_spec():
    return pl.BlockSpec(memory_space=pltpu.VMEM)


def after(value, *others):
    return lax.optimization_barrier((value, *others))[0]


def params():
    return pltpu.CompilerParams(dimension_semantics=("arbitrary",), vmem_limit_bytes=VMEM_LIMIT)


def packed_outs(z, sent_type):
    return (
        (
            jax.ShapeDtypeStruct((z.half_rows, z.all_tok), f32),
            jax.ShapeDtypeStruct((z.half_rows, z.all_tok), sent_type),
        ),
        (whole_spec((z.half_rows, z.all_tok)), whole_spec((z.half_rows, z.all_tok))),
    )


def cost(z, matmuls, extra=0):
    size = z.width * z.hidden
    return pl.CostEstimate(
        flops=int(2 * z.all_tok * size * matmuls),
        bytes_accessed=int(2 * size * matmuls + extra),
        transcendentals=0,
    )


def forward_part(z, lists, lane_group, pieces, weight, sent_type, waits):
    tile = tile_of(z.hidden, 512, 256, 128)
    steps = z.hidden // tile

    def kernel(lists_ref, group_ref, *refs):
        piece_refs, refs = refs[: z.cols], refs[z.cols :]
        w_ref, mine, theirs, rows, dense = refs[:1] + refs[1 + len(waits) :]
        i = pl.program_id(0)

        @pl.when(i == 0)
        def _():
            z.assemble(piece_refs, rows)
            dense[z.hidden : z.hidden + BLK, :] = jnp.zeros((BLK, z.all_tok), f32)

        part = jnp.dot(rows[...], w_ref[...], preferred_element_type=f32)
        dense[pl.ds(pl.multiple_of(i * tile, tile), tile), :] = part.T

        @pl.when(i == steps - 1)
        def _():
            z.pack(lists_ref, group_ref, dense, mine, theirs)

    out_shape, out_specs = packed_outs(z, sent_type)
    return pl.pallas_call(
        kernel,
        out_shape=out_shape,
        grid_spec=pltpu.PrefetchScalarGridSpec(
            num_scalar_prefetch=1,
            grid=(steps,),
            in_specs=[whole_spec(lane_group.shape)]
            + [whole_spec(piece.shape) for piece in pieces]
            + [pl.BlockSpec((None, z.width, tile), lambda i, *_: (0, 0, i))]
            + [any_spec()] * len(waits),
            out_specs=out_specs,
            scratch_shapes=[
                pltpu.VMEM((z.all_tok, z.width), bf16),
                pltpu.VMEM((z.hidden + BLK, z.all_tok), f32),
            ],
        ),
        compiler_params=params(),
        cost_estimate=cost(z, 1),
    )(lists, lane_group, *pieces, weight, *waits)


def back_part(z, lists, lane_group, pieces, weight, chunk, chunks, before, waits):
    tile = tile_of(z.hidden, 512, 256, 128)
    steps = z.hidden // tile
    extent = z.width // chunks
    last = chunk == chunks - 1

    def kernel(lists_ref, group_ref, *refs):
        piece_refs, refs = refs[: z.cols], refs[z.cols :]
        w_ref, refs = refs[0], refs[1:]
        if before is not None:
            before_ref, refs = refs[0], refs[1:]
        refs = refs[len(waits) :]
        i = pl.program_id(0)
        rows = refs[-1] if not last else refs[-2]

        @pl.when(i == 0)
        def _():
            z.assemble(piece_refs, rows)

        part = lax.dot_general(
            w_ref[...], rows[...], (((1,), (1,)), ((), ())), preferred_element_type=f32
        )
        if before is not None:
            part = part + before_ref[...]
        if not last:
            refs[0][...] = part
        else:
            mine, theirs, _, dense = refs
            dense[pl.ds(pl.multiple_of(i * tile, tile), tile), :] = part

            @pl.when(i == steps - 1)
            def _():
                dense[z.hidden : z.hidden + BLK, :] = jnp.zeros((BLK, z.all_tok), f32)
                z.pack(lists_ref, group_ref, dense, mine, theirs)

    scratch = [pltpu.VMEM((z.all_tok, extent), bf16)]
    row_spec = pl.BlockSpec((tile, z.all_tok), lambda i, *_: (i, 0))
    if last:
        out_shape, out_specs = packed_outs(z, bf16)
        scratch.append(pltpu.VMEM((z.hidden + BLK, z.all_tok), f32))
    else:
        out_shape, out_specs = jax.ShapeDtypeStruct((z.hidden, z.all_tok), f32), row_spec
    ins = [lane_group, *pieces, weight]
    in_specs = (
        [whole_spec(lane_group.shape)]
        + [whole_spec(piece.shape) for piece in pieces]
        + [pl.BlockSpec((None, tile, extent), lambda i, *_: (0, i, chunk))]
    )
    if before is not None:
        ins.append(before)
        in_specs.append(row_spec)
    ins.extend(waits)
    in_specs.extend([any_spec()] * len(waits))
    return pl.pallas_call(
        kernel,
        out_shape=out_shape,
        grid_spec=pltpu.PrefetchScalarGridSpec(
            num_scalar_prefetch=1,
            grid=(steps,),
            in_specs=in_specs,
            out_specs=out_specs,
            scratch_shapes=scratch,
        ),
        compiler_params=params(),
        cost_estimate=cost(z, 1 / chunks),
    )(lists, *ins)


def spread_pair(z, places, lane_group, gate_halves, up_halves):
    def kernel(places_ref, group_ref, gm, gt, um, ut, dense_g, dense_u, packed_g, packed_u):
        z.join(gm, gt, packed_g)
        z.join(um, ut, packed_u)
        z.spread(places_ref, group_ref, [packed_g, packed_u], [dense_g, dense_u])

    return pl.pallas_call(
        kernel,
        out_shape=[jax.ShapeDtypeStruct((z.hidden, z.all_tok), bf16)] * 2,
        grid_spec=pltpu.PrefetchScalarGridSpec(
            num_scalar_prefetch=1,
            grid=(),
            in_specs=[vmem_spec()] * 5,
            out_specs=[vmem_spec()] * 2,
            scratch_shapes=[pltpu.VMEM((z.packed + BLK, z.all_tok), bf16)] * 2,
        ),
        compiler_params=pltpu.CompilerParams(vmem_limit_bytes=VMEM_LIMIT),
    )(places, lane_group, *gate_halves, *up_halves)


def sent_part(z, dense_gate, dense_up, w_gate, w_up, chunk, chunks, own_type):
    extent = z.width // chunks
    tile = tile_of(extent, 256, 128)
    steps = extent // tile

    def kernel(dense_g, dense_u, wg, wu, *outs):
        part = jnp.dot(wg[...], dense_g[...], preferred_element_type=f32)
        part = part + jnp.dot(wu[...], dense_u[...], preferred_element_type=f32)
        turned = part.T
        for m in range(z.micro):
            for k in range(z.cols):
                start = m * z.tok + k * z.local
                outs[k][m] = turned[start : start + z.local, :].astype(outs[k].dtype)

    w_spec = pl.BlockSpec((None, tile, z.hidden), lambda i: (0, chunk * steps + i, 0))
    out_spec = pl.BlockSpec((z.micro, z.local, tile), lambda i: (0, 0, i))
    return pl.pallas_call(
        kernel,
        out_shape=[
            jax.ShapeDtypeStruct((z.micro, z.local, extent), own_type if k == 0 else bf16)
            for k in range(z.cols)
        ],
        grid=(steps,),
        in_specs=[vmem_spec()] * 2 + [w_spec, w_spec],
        out_specs=[out_spec] * z.cols,
        compiler_params=params(),
        cost_estimate=cost(z, 2 / chunks),
    )(dense_gate, dense_up, w_gate, w_up)


def down_gradient(z, places, lane_group, halves, chunk_pieces):
    tile = tile_of(z.hidden, 512, 256, 128)
    steps = z.hidden // tile
    flat = [piece for pieces in chunk_pieces for piece in pieces]
    count = len(flat)

    def kernel(places_ref, group_ref, hm, ht, *refs):
        piece_refs, (out, packed, dense, rows) = refs[:count], refs[count:]
        i = pl.program_id(0)

        @pl.when(i == 0)
        def _():
            z.join(hm, ht, packed)
            z.spread(places_ref, group_ref, [packed], [dense])
            for n in range(len(chunk_pieces)):
                group = piece_refs[n * z.cols : (n + 1) * z.cols]
                z.assemble(group, rows, n * group[0].shape[-1])

        own = dense[pl.ds(pl.multiple_of(i * tile, tile), tile), :]
        out[...] = jnp.dot(own, rows[...], preferred_element_type=f32).astype(bf16)

    half = (z.half_rows, z.all_tok)
    return pl.pallas_call(
        kernel,
        out_shape=jax.ShapeDtypeStruct((1, z.hidden, z.width), bf16),
        grid_spec=pltpu.PrefetchScalarGridSpec(
            num_scalar_prefetch=1,
            grid=(steps,),
            in_specs=[whole_spec(lane_group.shape)]
            + [whole_spec(half)] * 2
            + [whole_spec(piece.shape) for piece in flat],
            out_specs=pl.BlockSpec((None, tile, z.width), lambda i, *_: (0, i, 0)),
            scratch_shapes=[
                pltpu.VMEM((z.packed + BLK, z.all_tok), bf16),
                pltpu.VMEM((z.hidden, z.all_tok), bf16),
                pltpu.VMEM((z.all_tok, z.width), bf16),
            ],
        ),
        compiler_params=params(),
        cost_estimate=cost(z, 1),
    )(places, lane_group, *halves, *flat)


def gate_up_gradients(z, dense_gate, dense_up, pieces, waits):
    tile = tile_of(z.width, 256, 128)
    steps = z.width // tile

    def kernel(dense_g, dense_u, *refs):
        piece_refs, refs = refs[: z.cols], refs[z.cols :]
        out_g, out_u, rows = refs[len(waits) :]
        z.assemble(piece_refs, rows)
        turned = rows[...].T
        dims = (((1,), (1,)), ((), ()))
        out_g[...] = lax.dot_general(
            turned, dense_g[...], dims, preferred_element_type=f32
        ).astype(bf16)
        out_u[...] = lax.dot_general(
            turned, dense_u[...], dims, preferred_element_type=f32
        ).astype(bf16)

    out_spec = pl.BlockSpec((None, tile, z.hidden), lambda i: (0, i, 0))
    return pl.pallas_call(
        kernel,
        out_shape=[jax.ShapeDtypeStruct((1, z.width, z.hidden), bf16)] * 2,
        grid=(steps,),
        in_specs=[vmem_spec()] * 2
        + [pl.BlockSpec((z.micro, z.local, tile), lambda i: (0, 0, i))] * z.cols
        + [any_spec()] * len(waits),
        out_specs=[out_spec] * 2,
        scratch_shapes=[pltpu.VMEM((z.all_tok, tile), bf16)],
        compiler_params=params(),
        cost_estimate=cost(z, 2),
    )(dense_gate, dense_up, *pieces, *waits)


def core_total(parts):
    mine, theirs = parts
    chip = mine + swapped(theirs, "row").astype(f32)
    return chip, chip.astype(bf16)


def row_total(chip, outgoing, *others):
    total = chip
    for step in range(2, lax.axis_size("row"), 2):
        arrived = rotated(outgoing, "row", step)
        if others:
            arrived = after(arrived, *others)
        total = total + arrived.astype(f32)
    return total


def handed_rows(z, is_last, top, arrived, chunk, chunks):
    extent = z.width // chunks

    def kernel(flag, top_ref, *refs):
        arrived_refs, out = refs[:-1], refs[-1]
        own = top_ref[...]
        total = own.astype(f32)
        for ref in arrived_refs:
            total = total + ref[...].astype(f32)
        out[...] = jnp.where(flag[0] == 1, own, total.astype(bf16))

    shape = (z.micro, z.local, extent)
    return pl.pallas_call(
        kernel,
        out_shape=jax.ShapeDtypeStruct(shape, bf16),
        grid_spec=pltpu.PrefetchScalarGridSpec(
            num_scalar_prefetch=1,
            grid=(1,),
            in_specs=[pl.BlockSpec(shape, lambda i, *_: (0, 0, chunk))]
            + [whole_spec(shape)] * len(arrived),
            out_specs=whole_spec(shape),
        ),
        compiler_params=params(),
    )(is_last, top, *arrived)


def final_rows(z, chunk_terms):
    chunks = len(chunk_terms)
    extent = z.width // chunks
    count = len(chunk_terms[0])

    def kernel(*refs):
        out = refs[-1]
        for n in range(chunks):
            total = None
            for ref in refs[n * count : (n + 1) * count]:
                term = ref[...].astype(f32)
                total = term if total is None else total + term
            out[:, :, n * extent : (n + 1) * extent] = total.astype(bf16)

    shape = (z.micro, z.local, extent)
    return pl.pallas_call(
        kernel,
        out_shape=jax.ShapeDtypeStruct((1, z.micro, z.local, z.width), bf16),
        grid=(1,),
        in_specs=[whole_spec(shape)] * (chunks * count),
        out_specs=pl.BlockSpec((None, z.micro, z.local, z.width), lambda i: (0, 0, 0, 0)),
        compiler_params=params(),
    )(*[term for terms in chunk_terms for term in terms])


def handed_along(value):
    sections = lax.axis_size("section")
    return lax.ppermute(value, "section", [(i, i - 1) for i in range(1, sections)])


def straight_back(rows):
    sections, cols = lax.axis_size("section"), len(rows)
    arrived = []
    for k in range(cols):
        pairs = [
            (s * cols + c, (s - 1) * cols + (c - k) % cols)
            for s in range(1, sections)
            for c in range(cols)
        ]
        arrived.append(lax.ppermute(rows[k], ("section", "col"), pairs))
    return arrived


def shards(layer_input, top_grad, w_gate, w_up, w_down, activity):
    sections = lax.axis_size("section")
    is_last = lax.axis_index("section") == sections - 1
    cols = lax.axis_size("col")
    col = lax.axis_index("col")
    core = lax.axis_index("row") % 2
    inputs = layer_input[0]
    lists = activity[0, :, :, 0, :]
    z = Sizes(
        inputs.shape[0], inputs.shape[1], cols, inputs.shape[2], w_gate.shape[2], lists.shape[-1]
    )

    turned = jnp.where(core == 0, lists, jnp.roll(lists, -z.half, axis=-1))
    numbers = jnp.arange(z.blocks, dtype=jnp.int32)
    hit = turned[..., :, None] == numbers
    slot_ids = jnp.arange(z.slots, dtype=jnp.int32)[:, None]
    places = jnp.min(jnp.where(hit, slot_ids, z.slots), axis=-2).reshape(-1)
    turned = turned.reshape(-1)
    lane = jnp.arange(z.tok, dtype=jnp.int32)
    source = (col - lane // z.local) % cols
    group = (source * z.local + lane % z.local) // TB
    lane_group = jnp.broadcast_to(group[None], (8, z.tok))
    flag = is_last.astype(jnp.int32).reshape(1)

    input_pieces = gathered(inputs, "col")
    top_pieces = gathered(after(top_grad, *input_pieces), "col")
    gate_parts = forward_part(z, turned, lane_group, input_pieces, w_gate, f32, ())
    gate_chip = core_total(gate_parts)
    up_parts = forward_part(z, turned, lane_group, input_pieces, w_up, f32, gate_chip[1:])
    up_chip = core_total(up_parts)
    back_parts = back_part(
        z, turned, lane_group, top_pieces, w_down, 0, 1, None, up_chip[1:]
    )
    back_chip = core_total(back_parts)
    gate = row_total(*gate_chip)
    up = row_total(*up_chip)
    positive = jnp.maximum(gate, 0.0)
    squared = positive * positive
    slope = 2.0 * positive * up
    hidden = (squared * up).astype(bf16)
    hidden_halves = (hidden, swapped(hidden, "row"))

    extent = z.width // CHUNKS
    spans = [slice(n * extent, (n + 1) * extent) for n in range(CHUNKS)]
    own = [top_grad[:, :, span] for span in spans]
    chunk_pieces = [top_pieces]
    for turn in range(sections):
        final = turn == sections - 1
        if turn > 0:
            chunk_pieces = []
            for n in range(CHUNKS):
                chunk_pieces.append(gathered(own[n], "col"))
            back_parts = None
            for n in range(CHUNKS):
                back_parts = back_part(
                    z, turned, lane_group, chunk_pieces[n], w_down, n, CHUNKS, back_parts, ()
                )
            back_chip = core_total(back_parts)
        others = ()
        if final:
            down_grad = down_gradient(z, places, lane_group, hidden_halves, chunk_pieces)
            others = (down_grad,)
        back = row_total(*back_chip, *others)
        grad_gate = (slope * back).astype(bf16)
        grad_up = (squared * back).astype(bf16)
        gate_halves = (grad_gate, swapped(grad_gate, "row"))
        up_halves = (grad_up, swapped(grad_up, "row"))
        dense = spread_pair(z, places, lane_group, gate_halves, up_halves)
        chunk_terms, later = [], []
        for n in range(CHUNKS):
            own_type = bf16 if turn == 0 and not final else f32
            rows = sent_part(z, *dense, w_gate, w_up, n, CHUNKS, own_type)
            if turn == 0 and not final:
                arrived = straight_back(rows)
            else:
                arrived = [rotated(rows[k], "col", -k) for k in range(1, cols)]
            if final:
                chunk_terms.append([own[n], rows[0], *arrived])
            elif turn == 0:
                later.append(handed_rows(z, flag, top_grad, arrived, n, CHUNKS))
            else:
                total = sum((row.astype(f32) for row in arrived), own[n].astype(f32) + rows[0])
                passed = handed_along(total.astype(bf16))
                later.append(jnp.where(is_last, top_grad[:, :, spans[n]], passed))
        own = later
    gate_grad, up_grad = gate_up_gradients(z, *dense, input_pieces, ())
    return final_rows(z, chunk_terms), gate_grad, up_grad, down_grad


def solution(mesh):
    in_specs = (
        P("section", None, "col", "row"),
        P(None, "col", "row"),
        P("section", "row", "col"),
        P("section", "row", "col"),
        P("section", "col", "row"),
        P("section", None, None, "col", None),
    )
    out_specs = (
        P("section", None, "col", "row"),
        P("section", "row", "col"),
        P("section", "row", "col"),
        P("section", "col", "row"),
    )
    return jax.shard_map(shards, mesh=mesh, in_specs=in_specs, out_specs=out_specs, check_vma=False)
```

```python
import jax
import jax.numpy as jnp
from jax import lax
from jax.experimental import pallas as pl
from jax.experimental.pallas import tpu as pltpu
from jax.sharding import PartitionSpec as P


BLK = 64
TB = 64
CHUNKS = 2
DEPTH = 3
VMEM_LIMIT = 48 * 1024 * 1024

bf16 = jnp.bfloat16
f32 = jnp.float32


def rotated(value, axis, steps):
    count = lax.axis_size(axis)
    return lax.ppermute(value, axis, [(i, (i + steps) % count) for i in range(count)])


def swapped(value, axis):
    count = lax.axis_size(axis)
    return lax.ppermute(value, axis, [(i, i ^ 1) for i in range(count)])


def gathered(value, axis):
    count = lax.axis_size(axis)
    return [value] + [rotated(value, axis, k) for k in range(1, count)]


def tile_of(extent, *choices):
    for choice in choices:
        if extent % choice == 0:
            return choice
    return extent


class Sizes:
    def __init__(self, micro, local, cols, width, hidden, slots):
        self.micro, self.local, self.cols = micro, local, cols
        self.width, self.hidden, self.slots = width, hidden, slots
        self.tok = local * cols
        self.all_tok = micro * self.tok
        self.groups = self.tok // TB
        self.blocks = hidden // BLK
        self.half = slots // 2
        self.packed = slots * BLK
        self.half_rows = self.half * BLK

    def assemble(self, pieces, dest, first=0):
        extent = pieces[0].shape[-1]
        for m in range(self.micro):
            for k in range(self.cols):
                start = m * self.tok + k * self.local
                dest[start : start + self.local, first : first + extent] = pieces[k][m]

    def pack(self, lists, lane_group, dense, mine, theirs):
        masks = [
            jnp.broadcast_to(lane_group[0:1, :] == g, (BLK, self.tok)) for g in range(1, self.groups)
        ]

        def one(j, dest):
            def step(slot, carry):
                for m in range(self.micro):
                    lanes = slice(m * self.tok, (m + 1) * self.tok)
                    value = None
                    for g in range(self.groups):
                        block = lists[(m * self.groups + g) * self.slots + j * self.half + slot]
                        rows = pl.ds(pl.multiple_of(block * BLK, BLK), BLK)
                        part = dense[rows, lanes]
                        value = part if value is None else jnp.where(masks[g - 1], part, value)
                    out_rows = pl.ds(pl.multiple_of(slot * BLK, BLK), BLK)
                    dest[out_rows, lanes] = value.astype(dest.dtype)
                return carry

            lax.fori_loop(0, self.half, step, 0, unroll=7)

        one(0, mine)
        one(1, theirs)

    def spread(self, places, lane_group, packed_list, dense_list):
        masks = [
            jnp.broadcast_to(lane_group[0:1, :] == g, (BLK, self.tok)) for g in range(1, self.groups)
        ]

        def step(block, carry):
            for m in range(self.micro):
                lanes = slice(m * self.tok, (m + 1) * self.tok)
                rows = []
                for g in range(self.groups):
                    place = places[(m * self.groups + g) * self.blocks + block]
                    rows.append(pl.ds(pl.multiple_of(place * BLK, BLK), BLK))
                out_rows = pl.ds(pl.multiple_of(block * BLK, BLK), BLK)
                for packed, dense in zip(packed_list, dense_list):
                    value = packed[rows[0], lanes]
                    for g in range(1, self.groups):
                        value = jnp.where(masks[g - 1], packed[rows[g], lanes], value)
                    dense[out_rows, lanes] = value
            return carry

        lax.fori_loop(0, self.blocks, step, 0, unroll=4)

    def join(self, mine, theirs, packed):
        packed[0 : self.half_rows, :] = mine[...]
        packed[self.half_rows : self.packed, :] = theirs[...]
        packed[self.packed : self.packed + BLK, :] = jnp.zeros((BLK, self.all_tok), packed.dtype)


def whole_spec(shape):
    zeros = (0,) * len(shape)
    return pl.BlockSpec(shape, lambda *_: zeros)


def any_spec():
    return pl.BlockSpec(memory_space=pl.ANY)


def hbm_spec():
    return pl.BlockSpec(memory_space=pltpu.HBM)


def vmem_spec():
    return pl.BlockSpec(memory_space=pltpu.VMEM)


def after(value, *others):
    return lax.optimization_barrier((value, *others))[0]


def params():
    return pltpu.CompilerParams(dimension_semantics=("arbitrary",), vmem_limit_bytes=VMEM_LIMIT)


def packed_outs(z, sent_type):
    return [
        jax.ShapeDtypeStruct((z.half_rows, z.all_tok), f32),
        jax.ShapeDtypeStruct((z.half_rows, z.all_tok), sent_type),
    ]


def cost(z, matmuls, extra=0):
    size = z.width * z.hidden
    return pl.CostEstimate(
        flops=int(2 * z.all_tok * size * matmuls),
        bytes_accessed=int(2 * size * matmuls + extra),
        transcendentals=0,
    )


def stream(total, depth, copies, use):
    def begin(i, slot):
        for copy in copies(i, slot):
            copy.start()

    for i in range(min(depth, total)):
        begin(i, i)

    def step(i, carry):
        slot = lax.rem(i, depth)
        for copy in copies(i, slot):
            copy.wait()
        use(i, slot)

        @pl.when(i + depth < total)
        def _():
            begin(i + depth, slot)

        return carry

    return lambda: lax.fori_loop(0, total, step, 0)


def piece_copies(z, pieces, rows, sems):
    copies = []
    for m in range(z.micro):
        for k in range(z.cols):
            place = rows.at[pl.ds(m * z.tok + k * z.local, z.local), :]
            copies.append(
                pltpu.make_async_copy(pieces[k].at[m], place, sems.at[m * z.cols + k])
            )
    return copies


def tile_rows(i, tile):
    return pl.ds(pl.multiple_of(i * tile, tile), tile)


def plain_params():
    return pltpu.CompilerParams(vmem_limit_bytes=VMEM_LIMIT)


def forward_part(z, lists, lane_group, pieces, weight, sent_type, waits):
    tile = tile_of(z.hidden, 896, 512, 256, 128)

    def kernel(lists_ref, group_ref, *refs):
        piece_refs, w_ref = refs[: z.cols], refs[z.cols]
        mine, theirs, rows, dense, tiles, tile_sems, piece_sems = refs[z.cols + 1 + len(waits) :]

        def copies(i, slot):
            source = w_ref.at[0, :, tile_rows(i, tile)]
            return [pltpu.make_async_copy(source, tiles.at[slot], tile_sems.at[slot])]

        def use(i, slot):
            dense[tile_rows(i, tile), :] = lax.dot_general(
                tiles[slot], rows[...], (((0,), (1,)), ((), ())), preferred_element_type=f32
            )

        arriving = piece_copies(z, piece_refs, rows, piece_sems)
        for copy in arriving:
            copy.start()
        run = stream(z.hidden // tile, DEPTH, copies, use)
        dense[z.hidden : z.hidden + BLK, :] = jnp.zeros((BLK, z.all_tok), f32)
        for copy in arriving:
            copy.wait()
        run()
        z.pack(lists_ref, group_ref, dense, mine, theirs)

    return pl.pallas_call(
        kernel,
        out_shape=packed_outs(z, sent_type),
        grid_spec=pltpu.PrefetchScalarGridSpec(
            num_scalar_prefetch=1,
            grid=(),
            in_specs=[vmem_spec(), hbm_spec()] + [any_spec()] * (z.cols + len(waits)),
            out_specs=[vmem_spec()] * 2,
            scratch_shapes=[
                pltpu.VMEM((z.all_tok, z.width), bf16),
                pltpu.VMEM((z.hidden + BLK, z.all_tok), f32),
                pltpu.VMEM((DEPTH, z.width, tile), bf16),
                pltpu.SemaphoreType.DMA((DEPTH,)),
                pltpu.SemaphoreType.DMA((z.micro * z.cols,)),
            ],
        ),
        compiler_params=plain_params(),
        cost_estimate=cost(z, 1),
    )(lists, lane_group, *pieces, weight, *waits)


def back_part(z, lists, lane_group, pieces, weight, chunk, chunks, before, waits):
    tile = tile_of(z.hidden, 896, 512, 256, 128)
    extent = z.width // chunks
    last = chunk == chunks - 1
    earlier = [] if before is None else [before]

    def kernel(lists_ref, group_ref, *refs):
        before_refs, refs = refs[: len(earlier)], refs[len(earlier) :]
        piece_refs, w_ref = refs[: z.cols], refs[z.cols]
        refs = refs[z.cols + 1 + len(waits) :]
        if last:
            mine, theirs, rows, tiles, tile_sems, piece_sems, dense = refs
        else:
            dense, rows, tiles, tile_sems, piece_sems = refs

        def copies(i, slot):
            source = w_ref.at[0, tile_rows(i, tile), pl.ds(chunk * extent, extent)]
            return [pltpu.make_async_copy(source, tiles.at[slot], tile_sems.at[slot])]

        def use(i, slot):
            part = lax.dot_general(
                tiles[slot], rows[...], (((1,), (1,)), ((), ())), preferred_element_type=f32
            )
            for ref in before_refs:
                part = part + ref[tile_rows(i, tile), :]
            dense[tile_rows(i, tile), :] = part

        arriving = piece_copies(z, piece_refs, rows, piece_sems)
        for copy in arriving:
            copy.start()
        run = stream(z.hidden // tile, DEPTH, copies, use)
        for copy in arriving:
            copy.wait()
        run()
        if last:
            dense[z.hidden : z.hidden + BLK, :] = jnp.zeros((BLK, z.all_tok), f32)
            z.pack(lists_ref, group_ref, dense, mine, theirs)

    scratch = [
        pltpu.VMEM((z.all_tok, extent), bf16),
        pltpu.VMEM((DEPTH, tile, extent), bf16),
        pltpu.SemaphoreType.DMA((DEPTH,)),
        pltpu.SemaphoreType.DMA((z.micro * z.cols,)),
    ]
    if last:
        out_shape, out_specs = packed_outs(z, bf16), [vmem_spec()] * 2
        scratch.append(pltpu.VMEM((z.hidden + BLK, z.all_tok), f32))
    else:
        out_shape = jax.ShapeDtypeStruct((z.hidden, z.all_tok), f32)
        out_specs = vmem_spec()
    return pl.pallas_call(
        kernel,
        out_shape=out_shape,
        grid_spec=pltpu.PrefetchScalarGridSpec(
            num_scalar_prefetch=1,
            grid=(),
            in_specs=[vmem_spec()] * (1 + len(earlier))
            + [hbm_spec() if chunks == 1 else any_spec()]
            + [any_spec()] * (z.cols + len(waits)),
            out_specs=out_specs,
            scratch_shapes=scratch,
        ),
        compiler_params=plain_params(),
        cost_estimate=cost(z, 1 / chunks),
    )(lists, lane_group, *earlier, *pieces, weight, *waits)


def spread_pair(z, places, lane_group, gate_halves, up_halves):
    def kernel(places_ref, group_ref, gm, gt, um, ut, dense_g, dense_u, packed_g, packed_u):
        z.join(gm, gt, packed_g)
        z.join(um, ut, packed_u)
        z.spread(places_ref, group_ref, [packed_g, packed_u], [dense_g, dense_u])

    return pl.pallas_call(
        kernel,
        out_shape=[jax.ShapeDtypeStruct((z.hidden, z.all_tok), bf16)] * 2,
        grid_spec=pltpu.PrefetchScalarGridSpec(
            num_scalar_prefetch=1,
            grid=(),
            in_specs=[vmem_spec()] * 5,
            out_specs=[vmem_spec()] * 2,
            scratch_shapes=[pltpu.VMEM((z.packed + BLK, z.all_tok), bf16)] * 2,
        ),
        compiler_params=pltpu.CompilerParams(vmem_limit_bytes=VMEM_LIMIT),
    )(places, lane_group, *gate_halves, *up_halves)


def sent_part(z, dense_gate, dense_up, w_gate, w_up, chunk, chunks):
    extent = z.width // chunks
    tile = tile_of(extent, 256, 128)

    def kernel(dense_g, dense_u, wg, wu, *refs):
        outs, (tiles_g, tiles_u, sems) = refs[: z.cols], refs[z.cols :]

        def copies(i, slot):
            rows = pl.ds(pl.multiple_of(chunk * extent + i * tile, tile), tile)
            return [
                pltpu.make_async_copy(wg.at[0, rows, :], tiles_g.at[slot], sems.at[0, slot]),
                pltpu.make_async_copy(wu.at[0, rows, :], tiles_u.at[slot], sems.at[1, slot]),
            ]

        def use(i, slot):
            part = jnp.dot(tiles_g[slot], dense_g[...], preferred_element_type=f32)
            part = part + jnp.dot(tiles_u[slot], dense_u[...], preferred_element_type=f32)
            turned = part.T
            for m in range(z.micro):
                for k in range(z.cols):
                    start = m * z.tok + k * z.local
                    outs[k][m, :, tile_rows(i, tile)] = turned[start : start + z.local, :].astype(
                        outs[k].dtype
                    )

        stream(extent // tile, 3, copies, use)()

    return pl.pallas_call(
        kernel,
        out_shape=[
            jax.ShapeDtypeStruct((z.micro, z.local, extent), f32 if k == 0 else bf16)
            for k in range(z.cols)
        ],
        in_specs=[vmem_spec()] * 2 + [any_spec()] * 2,
        out_specs=[vmem_spec()] * z.cols,
        scratch_shapes=[pltpu.VMEM((3, tile, z.hidden), bf16)] * 2
        + [pltpu.SemaphoreType.DMA((2, 3))],
        compiler_params=plain_params(),
        cost_estimate=cost(z, 2 / chunks),
    )(dense_gate, dense_up, w_gate, w_up)


def down_gradient(z, places, lane_group, halves, chunk_pieces):
    tile = tile_of(z.hidden, 512, 256, 128)
    steps = z.hidden // tile
    flat = [piece for pieces in chunk_pieces for piece in pieces]
    count = len(flat)

    def kernel(places_ref, group_ref, hm, ht, *refs):
        piece_refs, (out, packed, dense, rows) = refs[:count], refs[count:]
        i = pl.program_id(0)

        @pl.when(i == 0)
        def _():
            z.join(hm, ht, packed)
            z.spread(places_ref, group_ref, [packed], [dense])
            for n in range(len(chunk_pieces)):
                group = piece_refs[n * z.cols : (n + 1) * z.cols]
                z.assemble(group, rows, n * group[0].shape[-1])

        own = dense[pl.ds(pl.multiple_of(i * tile, tile), tile), :]
        out[...] = jnp.dot(own, rows[...], preferred_element_type=f32).astype(bf16)

    half = (z.half_rows, z.all_tok)
    return pl.pallas_call(
        kernel,
        out_shape=jax.ShapeDtypeStruct((1, z.hidden, z.width), bf16),
        grid_spec=pltpu.PrefetchScalarGridSpec(
            num_scalar_prefetch=1,
            grid=(steps,),
            in_specs=[whole_spec(lane_group.shape)]
            + [whole_spec(half)] * 2
            + [whole_spec(piece.shape) for piece in flat],
            out_specs=pl.BlockSpec((None, tile, z.width), lambda i, *_: (0, i, 0)),
            scratch_shapes=[
                pltpu.VMEM((z.packed + BLK, z.all_tok), bf16),
                pltpu.VMEM((z.hidden, z.all_tok), bf16),
                pltpu.VMEM((z.all_tok, z.width), bf16),
            ],
        ),
        compiler_params=params(),
        cost_estimate=cost(z, 1),
    )(places, lane_group, *halves, *flat)


def gate_up_gradients(z, dense_gate, dense_up, pieces, waits):
    tile = tile_of(z.width, 256, 128)
    steps = z.width // tile

    def kernel(dense_g, dense_u, *refs):
        piece_refs, refs = refs[: z.cols], refs[z.cols :]
        out_g, out_u, rows = refs[len(waits) :]
        z.assemble(piece_refs, rows)
        turned = rows[...].T
        dims = (((1,), (1,)), ((), ()))
        out_g[...] = lax.dot_general(
            turned, dense_g[...], dims, preferred_element_type=f32
        ).astype(bf16)
        out_u[...] = lax.dot_general(
            turned, dense_u[...], dims, preferred_element_type=f32
        ).astype(bf16)

    out_spec = pl.BlockSpec((None, tile, z.hidden), lambda i: (0, i, 0))
    return pl.pallas_call(
        kernel,
        out_shape=[jax.ShapeDtypeStruct((1, z.width, z.hidden), bf16)] * 2,
        grid=(steps,),
        in_specs=[vmem_spec()] * 2
        + [pl.BlockSpec((z.micro, z.local, tile), lambda i: (0, 0, i))] * z.cols
        + [any_spec()] * len(waits),
        out_specs=[out_spec] * 2,
        scratch_shapes=[pltpu.VMEM((z.all_tok, tile), bf16)],
        compiler_params=params(),
        cost_estimate=cost(z, 2),
    )(dense_gate, dense_up, *pieces, *waits)


def core_total(parts):
    mine, theirs = parts
    chip = mine + swapped(theirs, "row").astype(f32)
    return chip, chip.astype(bf16)


def row_total(chip, outgoing, *others):
    total = chip
    for step in range(2, lax.axis_size("row"), 2):
        arrived = rotated(outgoing, "row", step)
        if others:
            arrived = after(arrived, *others)
        total = total + arrived.astype(f32)
    return total


def handed_rows(z, top, terms, chunk, chunks):
    extent = z.width // chunks

    def kernel(top_ref, *refs):
        term_refs, out = refs[:-1], refs[-1]
        total = top_ref[...].astype(f32)
        for ref in term_refs:
            total = total + ref[...].astype(f32)
        out[...] = total.astype(bf16)

    shape = (z.micro, z.local, extent)
    return pl.pallas_call(
        kernel,
        out_shape=jax.ShapeDtypeStruct(shape, bf16),
        grid=(1,),
        in_specs=[pl.BlockSpec(shape, lambda i: (0, 0, chunk))] + [vmem_spec()] * len(terms),
        out_specs=vmem_spec(),
        compiler_params=params(),
    )(top, *terms)


def chosen_rows(z, flag, top, passed, chunk, chunks):
    shape = (z.micro, z.local, z.width // chunks)

    def kernel(flag_ref, top_ref, passed_ref, out):
        out[...] = jnp.where(flag_ref[0] == 1, top_ref[...], passed_ref[...])

    return pl.pallas_call(
        kernel,
        out_shape=jax.ShapeDtypeStruct(shape, bf16),
        grid_spec=pltpu.PrefetchScalarGridSpec(
            num_scalar_prefetch=1,
            grid=(1,),
            in_specs=[pl.BlockSpec(shape, lambda i, *_: (0, 0, chunk)), vmem_spec()],
            out_specs=vmem_spec(),
        ),
        compiler_params=params(),
    )(flag, top, passed)


def final_rows(z, chunk_terms):
    chunks = len(chunk_terms)
    extent = z.width // chunks
    count = len(chunk_terms[0])

    def kernel(*refs):
        out = refs[-1]
        for n in range(chunks):
            total = None
            for ref in refs[n * count : (n + 1) * count]:
                term = ref[...].astype(f32)
                total = term if total is None else total + term
            out[:, :, n * extent : (n + 1) * extent] = total.astype(bf16)

    shape = (z.micro, z.local, extent)
    return pl.pallas_call(
        kernel,
        out_shape=jax.ShapeDtypeStruct((1, z.micro, z.local, z.width), bf16),
        grid=(1,),
        in_specs=[whole_spec(shape)] * (chunks * count),
        out_specs=pl.BlockSpec((None, z.micro, z.local, z.width), lambda i: (0, 0, 0, 0)),
        compiler_params=params(),
    )(*[term for terms in chunk_terms for term in terms])


def handed_along(value):
    sections = lax.axis_size("section")
    return lax.ppermute(value, "section", [(i, i - 1) for i in range(1, sections)])


def shards(layer_input, top_grad, w_gate, w_up, w_down, activity):
    sections = lax.axis_size("section")
    flag = (lax.axis_index("section") == sections - 1).astype(jnp.int32).reshape(1)
    cols = lax.axis_size("col")
    col = lax.axis_index("col")
    core = lax.axis_index("row") % 2
    inputs = layer_input[0]
    lists = activity[0, :, :, 0, :]
    z = Sizes(
        inputs.shape[0], inputs.shape[1], cols, inputs.shape[2], w_gate.shape[2], lists.shape[-1]
    )

    turned = jnp.where(core == 0, lists, jnp.roll(lists, -z.half, axis=-1))
    numbers = jnp.arange(z.blocks, dtype=jnp.int32)
    hit = turned[..., :, None] == numbers
    slot_ids = jnp.arange(z.slots, dtype=jnp.int32)[:, None]
    places = jnp.min(jnp.where(hit, slot_ids, z.slots), axis=-2).reshape(-1)
    turned = turned.reshape(-1)
    lane = jnp.arange(z.tok, dtype=jnp.int32)
    source = (col - lane // z.local) % cols
    group = (source * z.local + lane % z.local) // TB
    lane_group = jnp.broadcast_to(group[None], (8, z.tok))

    input_pieces = gathered(inputs, "col")
    top_pieces = gathered(after(top_grad, *input_pieces), "col")
    gate_parts = forward_part(z, turned, lane_group, input_pieces, w_gate, f32, ())
    gate_chip = core_total(gate_parts)
    up_parts = forward_part(z, turned, lane_group, input_pieces, w_up, f32, gate_chip[1:])
    up_chip = core_total(up_parts)
    back_parts = back_part(
        z, turned, lane_group, top_pieces, w_down, 0, 1, None, up_chip[1:]
    )
    back_chip = core_total(back_parts)
    gate = row_total(*gate_chip)
    up = row_total(*up_chip)
    positive = jnp.maximum(gate, 0.0)
    squared = positive * positive
    slope = 2.0 * positive * up
    hidden = (squared * up).astype(bf16)
    hidden_halves = (hidden, swapped(hidden, "row"))

    extent = z.width // CHUNKS
    spans = [slice(n * extent, (n + 1) * extent) for n in range(CHUNKS)]
    own = [top_grad[:, :, span] for span in spans]
    chunk_pieces = [top_pieces]
    for turn in range(sections):
        final = turn == sections - 1
        if turn > 0:
            chunk_pieces = []
            for n in range(CHUNKS):
                chunk_pieces.append(gathered(own[n], "col"))
            back_parts = None
            for n in range(CHUNKS):
                back_parts = back_part(
                    z, turned, lane_group, chunk_pieces[n], w_down, n, CHUNKS, back_parts, ()
                )
            back_chip = core_total(back_parts)
        others = ()
        if final:
            down_grad = down_gradient(z, places, lane_group, hidden_halves, chunk_pieces)
            others = (down_grad,)
        back = row_total(*back_chip, *others)
        grad_gate = (slope * back).astype(bf16)
        grad_up = (squared * back).astype(bf16)
        gate_halves = (grad_gate, swapped(grad_gate, "row"))
        up_halves = (grad_up, swapped(grad_up, "row"))
        dense = spread_pair(z, places, lane_group, gate_halves, up_halves)
        chunk_terms, later = [], []
        for n in range(CHUNKS):
            rows = sent_part(z, *dense, w_gate, w_up, n, CHUNKS)
            arrived = [rotated(rows[k], "col", -k) for k in range(1, cols)]
            if final:
                chunk_terms.append([own[n], rows[0], *arrived])
            else:
                if turn == 0:
                    total = handed_rows(z, top_grad, [rows[0], *arrived], n, CHUNKS)
                else:
                    total = own[n].astype(f32) + rows[0]
                    total = sum((row.astype(f32) for row in arrived), total).astype(bf16)
                passed = handed_along(total)
                later.append(chosen_rows(z, flag, top_grad, passed, n, CHUNKS))
        own = later
    gate_grad, up_grad = gate_up_gradients(z, *dense, input_pieces, ())
    return final_rows(z, chunk_terms), gate_grad, up_grad, down_grad


def solution(mesh):
    in_specs = (
        P("section", None, "col", "row"),
        P(None, "col", "row"),
        P("section", "row", "col"),
        P("section", "row", "col"),
        P("section", "col", "row"),
        P("section", None, None, "col", None),
    )
    out_specs = (
        P("section", None, "col", "row"),
        P("section", "row", "col"),
        P("section", "row", "col"),
        P("section", "col", "row"),
    )
    return jax.shard_map(shards, mesh=mesh, in_specs=in_specs, out_specs=out_specs, check_vma=False)
```
